256 devices in a mesh: cfg: 2 (over core), req: 16 (over x_hi, z), seq: 8 (over x_lo, y).
Axes of the slice: x: 4 (x_hi: 2, x_lo: 2; x = x_hi * 2 + x_lo), y: 4, z: 8, core: 2. Of those that a mesh axis runs over, the one named last changes fastest.
Arguments:
- hidden: bfloat16 [2, 16, 2304, 1536], P('cfg', 'req', 'seq'), may hold values from -6 to 6
- latent: float32 [16, 2304, 64], P('req', 'seq', 'cfg'), may hold values from -6 to 6
- modulation: float32 [16, 5, 1536], P('req'), may hold values from -3 to 3
- w_qkv: bfloat16 [1536, 4608], P('req'), may hold values from -1 to 1
- w_out: bfloat16 [1536, 1536], P('req'), may hold values from -0.15625 to 0.15625
- q_gain: float32 [1536], replicated, may hold values from 0 to 2
- k_gain: float32 [1536], replicated, may hold values from 0 to 2
- w_head: bfloat16 [1536, 64], replicated, may hold values from -0.15625 to 0.15625
- lengths: int32 [16], P('req'), may hold values from 288 to 2304, as said below
- guidance: float32 [16], P('req'), may hold values from 3 to 7
- step_size: float32 [16], P('req'), may hold values from 0.03 to 0.3
Outputs:
- new_latent: float32 [16, 2304, 64], P('req', 'seq', 'cfg')
The draws below stay inside these ranges and needn't reach their ends.
Inputs may be any that keep to these rules, and one draw needn't show every extreme that they name: `lengths`: some request has exactly 2304 video tokens in every draw.
All inputs are finite; a program needn't handle non-finite values.
Results may differ from the reference program's by a relative error of at most 0.01.
Values may be sent and summed in bfloat16 or wider, within the bound.
A program may use at most 128 MiB of HBM per device.

```python
import math
import jax
import jax.numpy as jnp
from jax import lax

D = 1536
H = 12
DH = 128
OUT = 64
TOK_DEV = 288
REQUESTS = 16
TOKENS = 2304


def draw_lengths(key, part):
    first, second = jax.random.split(jax.random.fold_in(key, 11))
    base = jax.random.randint(first, (REQUESTS,), TOK_DEV, TOKENS + 1)
    picked = jax.random.randint(second, (), 0, REQUESTS)
    return jnp.where(jnp.arange(REQUESTS) == picked, TOKENS, base).astype(jnp.int32)


def draw_hidden(key, part):
    noise_key = jax.random.fold_in(jax.random.fold_in(key, 21), 0)
    noise = jnp.clip(jax.random.normal(noise_key, (2, REQUESTS, TOKENS, D), jnp.float32), -6.0, 6.0)
    return noise.astype(jnp.bfloat16)


def draw_w_qkv(key, part):
    own_key = jax.random.fold_in(key, 31)
    return (jnp.clip(jax.random.normal(own_key, (D, 3 * D), jnp.float32), -6.0, 6.0) * D ** (-0.5)).astype(jnp.bfloat16)


def draw_q_gain(key, part):
    own_key = jax.random.fold_in(key, 41)
    return 1.0 + 0.15 * jnp.clip(jax.random.normal(own_key, (D,), jnp.float32), -5.0, 5.0)


def draw_k_gain(key, part):
    own_key = jax.random.fold_in(key, 43)
    return 1.0 + 0.15 * jnp.clip(jax.random.normal(own_key, (D,), jnp.float32), -5.0, 5.0)


def block_scale(key, extent, cuts, smallest, high):
    def one(dim, parts):
        draws = jax.random.uniform(jax.random.fold_in(jax.random.fold_in(key, 6), dim), (parts,), jnp.float32, smallest / len(cuts), high / len(cuts))
        return jnp.repeat(jnp.exp(draws), extent[dim] // parts).reshape((-1,) + (1,) * (len(extent) - dim - 1))

    level = one(*cuts[0])
    for cut in cuts[1:]:
        level = level * one(*cut)
    return level


def scatter_about(key, shape, scale, most, shards=(), held_as=jnp.bfloat16):
    array = scale * jax.random.normal(key, shape, jnp.float32)
    if shards:
        array = array * block_scale(key, shape, shards, -0.22, 0.18)
    return jnp.clip(array, -most, most).astype(held_as)


def setup_inputs(seed: int = 0) -> dict:
    key_list = jax.random.split(jax.random.key(seed), 12)
    hidden = draw_hidden(jax.random.fold_in(key_list[11], 71), 0)
    latent = scatter_about(key_list[1], (REQUESTS, TOKENS, OUT), 1.0, 6.0, ((0, 16), (1, 8), (2, 2)), jnp.float32)
    modulation = scatter_about(key_list[2], (REQUESTS, 5, D), 0.5, 3.0, ((0, 16),), jnp.float32)
    w_qkv = draw_w_qkv(jax.random.fold_in(key_list[11], 71), 0)
    w_out = scatter_about(key_list[4], (D, D), D ** -0.5, 0.15625, ((0, 16),))
    q_gain = draw_q_gain(jax.random.fold_in(key_list[11], 71), 0)
    k_gain = draw_k_gain(jax.random.fold_in(key_list[11], 71), 0)
    w_head = scatter_about(key_list[7], (D, OUT), D ** -0.5, 0.15625)
    lengths = draw_lengths(jax.random.fold_in(key_list[11], 71), 0)
    guidance = jnp.clip(3.0 + 4.0 * jax.random.uniform(key_list[9], (REQUESTS,), jnp.float32) ** block_scale(key_list[9], (REQUESTS,), ((0, 16),), -0.2, 0.2), 3.0, 7.0)
    step_size = jnp.clip(jnp.exp(math.log(0.3) - 2.3025852 * jax.random.uniform(key_list[10], (REQUESTS,), jnp.float32) ** block_scale(key_list[10], (REQUESTS,), ((0, 16),), -0.2, 0.2)), 0.03, 0.3)
    return {"hidden": hidden, "latent": latent, "modulation": modulation, "w_qkv": w_qkv, "w_out": w_out, "q_gain": q_gain, "k_gain": k_gain, "w_head": w_head, "lengths": lengths, "guidance": guidance, "step_size": step_size}


def layer_norm(values):
    centered = values - lax.optimization_barrier(jnp.mean(values, axis=-1, keepdims=True))
    return centered / jnp.sqrt(lax.optimization_barrier(jnp.mean(centered * centered, axis=-1, keepdims=True)) + 1e-06)

def rms_gain(values, gain):
    return values / jnp.sqrt(lax.optimization_barrier(jnp.mean(values * values, axis=-1, keepdims=True)) + 1e-06) * gain

def one_pass(state, modes, w_qkv, w_out, q_gain, k_gain, w_head, valid):
    width = state.shape[1]
    wide = state.astype(jnp.float32)
    normed = (layer_norm(wide) * (1.0 + modes[1]) + modes[0]).astype(jnp.bfloat16)
    qkv = jnp.dot(normed, w_qkv, preferred_element_type=jnp.float32)
    query = rms_gain(qkv[:, :width], q_gain).astype(jnp.bfloat16)
    keys = rms_gain(qkv[:, width:2 * width], k_gain).astype(jnp.bfloat16)
    values = qkv[:, 2 * width:].astype(jnp.bfloat16)
    rows = state.shape[0]
    query = query.reshape(rows, H, DH).astype(jnp.float32)
    keys = keys.reshape(rows, H, DH).astype(jnp.float32)
    values = values.reshape(rows, H, DH).astype(jnp.float32)
    scores = jnp.einsum('qhd,khd->qhk', query, keys) / jnp.sqrt(jnp.float32(DH))
    scores = jnp.where(valid[None, None, :], scores, jnp.float32(-1e+30))
    top = lax.optimization_barrier(jnp.max(scores, axis=-1, keepdims=True))
    probs = jnp.where(valid[None, None, :], jnp.exp(scores - top), jnp.float32(0.0))
    total = lax.optimization_barrier(jnp.sum(probs, axis=-1))
    weighted = jnp.einsum('qhk,khd->qhd', probs.astype(jnp.bfloat16).astype(jnp.float32), values)
    attended = (weighted / total[:, :, None]).reshape(rows, width).astype(jnp.bfloat16)
    projected = jnp.dot(attended, w_out, preferred_element_type=jnp.float32)
    block_out = (wide + modes[2] * projected).astype(jnp.bfloat16)
    head_in = (layer_norm(block_out.astype(jnp.float32)) * (1.0 + modes[4]) + modes[3]).astype(jnp.bfloat16)
    return jnp.dot(head_in, w_head, preferred_element_type=jnp.float32)

def reference(hidden, latent, modulation, w_qkv, w_out, q_gain, k_gain, w_head, lengths, guidance, step_size):

    def per_request(items):
        states, lat, modes, length, scale, step = items
        valid = jnp.arange(states.shape[1], dtype=jnp.int32) < length
        cond = one_pass(states[0], modes, w_qkv, w_out, q_gain, k_gain, w_head, valid)
        uncond = one_pass(states[1], modes, w_qkv, w_out, q_gain, k_gain, w_head, valid)
        guided = uncond + scale * (cond - uncond)
        return jnp.where(valid[:, None], lat - step * guided, lat)
    return lax.map(per_request, (jnp.transpose(hidden, (1, 0, 2, 3)), latent, modulation, lengths, guidance, step_size))
```

```python
import functools
import math

import jax
import jax.numpy as jnp
from jax import lax
from jax.experimental import pallas as pl
from jax.experimental.pallas import tpu as pltpu
from jax.sharding import PartitionSpec as P

MESH = pl.DeviceIdType.MESH
DH = 128
NY = 4
EPS = 1e-6
CH = 48


def norm_rows(x, scale, shift):
    c = x - jnp.mean(x, axis=-1, keepdims=True)
    return c * lax.rsqrt(jnp.mean(c * c, axis=-1, keepdims=True) + EPS) * (1.0 + scale) + shift


def kernel(
    NX,
    NZ,
    hid,
    wqkv,
    wout,
    mod,
    qg,
    kg,
    whead,
    length,
    guid,
    out,
    X,
    W,
    WO,
    xn,
    qk32,
    ssb,
    qbuf,
    kbuf,
    vbuf,
    att_s,
    att_r,
    acc,
    vsend,
    vrecv,
    bias,
    x_recv,
    t_send,
    y_send,
    w_recv,
    ring_send,
    share_send,
    xe_send,
    loc_sem,
    ss_send,
    ss_recv,
    kv_send,
    kv_recv,
    at_send,
    at_recv,
    v_send,
    v_recv,
):
    rows, width = hid.shape
    G = width // NY
    heads = G // DH
    HR = rows // 2
    R = NX * NZ
    half = NZ // 2
    k = lax.axis_index("cfg")
    r = lax.axis_index("req")
    s = lax.axis_index("seq")
    xh, z = r // NZ, r % NZ
    p, y = s // NY, s % NY

    def seq_of(a, b):
        return a * NY + b % NY

    yp = (k, r, seq_of(p, y + 1))
    ym = (k, r, seq_of(p, y + 3))
    y2 = (k, r, seq_of(p, y + 2))
    transposed = (p, r, k * NY + y)
    partner = (1 - k, r, s)
    xpart = (k, (1 - xh) * NZ + z, s)
    znext = (k, xh * NZ + (z + 1 + k * (NZ - 2)) % NZ, s)

    def remote(src, dst, ssem, rsem, dev):
        return pltpu.make_async_remote_copy(
            src_ref=src, dst_ref=dst, send_sem=ssem, recv_sem=rsem, device_id=dev, device_id_type=MESH
        )

    loc_w = [
        pltpu.make_async_copy(
            wqkv.at[:, pl.ds(pl.multiple_of(j * width + y * G, G), G)],
            W.at[r, :, pl.ds(j * G, G)],
            loc_sem.at[j],
        )
        for j in range(3)
    ]
    loc_wo = pltpu.make_async_copy(wout, WO.at[r], loc_sem.at[3])
    for c in loc_w:
        c.start()
    loc_wo.start()

    def hrows(h):
        return pl.ds(h * HR, HR)

    @pl.when(k == p)
    def _():
        for h in range(2):
            pltpu.make_async_copy(hid.at[hrows(h)], X.at[y, hrows(h)], x_recv.at[y, h]).start()

    barrier = pltpu.get_barrier_semaphore()
    peers = [
        yp,
        ym,
        y2,
        partner,
        (k, r, (1 - p) * NY + y),
        (1 - k, r, (1 - p) * NY + y),
    ]
    if NX > 1:
        peers.append(xpart)
    if NZ > 1:
        peers.append((k, xh * NZ + (z + 1) % NZ, s))
        peers.append((k, xh * NZ + (z + NZ - 1) % NZ, s))
    for dev in peers:
        pl.semaphore_signal(barrier, inc=1, device_id=dev, device_id_type=MESH)
    pl.semaphore_wait(barrier, len(peers))

    t_copies = [
        remote(hid.at[hrows(h)], X.at[y, hrows(h)], t_send.at[h], x_recv.at[y, h], transposed) for h in range(2)
    ]

    @pl.when(k != p)
    def _():
        for c in t_copies:
            c.start()

    bufs = (W, WO)

    def slot_at(side, t):
        other = xh if side == 0 else 1 - xh
        return other * NZ + (z + t * (NZ - 1) + k * 2 * t) % NZ

    def ring_copy(m, side, t):
        j = slot_at(side, t)
        return remote(bufs[m].at[j], bufs[m].at[j], ring_send.at[m, side, t], w_recv.at[m, j], znext)

    def share_copy(m, side, t):
        j = slot_at(side, t)
        return remote(bufs[m].at[j], bufs[m].at[j], share_send.at[m, side, t - 1], w_recv.at[m, j], partner)

    def mine(side):
        return (xh if side == 0 else 1 - xh) == k

    def recv_wait(m, j):
        pltpu.make_async_copy(bufs[m].at[j], bufs[m].at[j], w_recv.at[m, j]).wait()

    def ring_start(m, side):
        if NZ > 1:
            if half > 1:
                ring_copy(m, side, 0).start()
            else:

                @pl.when(mine(side))
                def _():
                    ring_copy(m, side, 0).start()

    def xe_copy(m):
        return remote(bufs[m].at[r], bufs[m].at[r], xe_send.at[m], w_recv.at[m, r], xpart)

    def ring_open(m):
        ring_start(m, 0)
        if NX > 1:
            xe_copy(m).start()

    def ring_second(m):
        if NX > 1:
            recv_wait(m, (1 - xh) * NZ + z)
            ring_start(m, 1)

    def ring_step(m, side, t):
        if NZ == 1 or t > half or side >= NX:
            return

        def go():
            recv_wait(m, slot_at(side, t))
            if t < half - 1:
                ring_copy(m, side, t).start()
            elif t == half - 1:

                @pl.when(mine(side))
                def _():
                    ring_copy(m, side, t).start()

            share_copy(m, side, t).start()

        if t < half:
            go()
        else:
            pl.when(mine(side))(go)

    def ring_shared(m):
        for side in range(NX):
            for t in range(half + 1, NZ):
                recv_wait(m, slot_at(side, t))
            if NZ > 1:

                @pl.when(jnp.logical_not(mine(side)))
                def _():
                    recv_wait(m, slot_at(side, half))

    def ring_drain(m):
        if NX > 1:
            xe_copy(m).wait_send()
        for side in range(NX):
            for t in range(half):
                if t < half - 1:
                    ring_copy(m, side, t).wait_send()
                else:

                    @pl.when(mine(side))
                    def _():
                        ring_copy(m, side, t).wait_send()

            for t in range(1, half + 1):
                if t < half:
                    share_copy(m, side, t).wait_send()
                else:

                    @pl.when(mine(side))
                    def _():
                        share_copy(m, side, t).wait_send()

    def x_copy(slot, h, n, dev):
        return remote(X.at[slot, hrows(h)], X.at[slot, hrows(h)], y_send.at[n], x_recv.at[slot, h], dev)

    def x_wait(slot, h):
        pltpu.make_async_copy(X.at[slot, hrows(h)], X.at[slot, hrows(h)], x_recv.at[slot, h]).wait()

    below, above, across = (y + 3) % NY, (y + 1) % NY, (y + 2) % NY
    x_sends = [
        x_copy(y, 0, 0, yp),
        x_copy(y, 1, 1, ym),
        x_copy(y, 1, 2, yp),
        x_copy(y, 0, 3, ym),
        x_copy(below, 0, 4, yp),
        x_copy(above, 1, 5, ym),
    ]

    def layer_in(slot):
        def chunk(i, carry):
            at = pl.ds(pl.multiple_of(i * CH, CH), CH)
            x = X[slot, at, :].astype(jnp.float32)
            xn[at, :] = norm_rows(x, mod[1:2, :], mod[0:1, :]).astype(jnp.bfloat16)
            return carry

        lax.fori_loop(0, rows // CH, chunk, 0)

    lanes = lax.broadcasted_iota(jnp.int32, (rows, DH), 1)

    def project(slot):
        qkv = jnp.dot(xn[...], W[...].reshape(width, 3 * G), preferred_element_type=jnp.float32)
        q = qkv[:, :G]
        kk = qkv[:, G : 2 * G]
        qk32[slot] = qkv[:, : 2 * G]
        sq = jnp.sum(q * q, axis=1, keepdims=True)
        sk = jnp.sum(kk * kk, axis=1, keepdims=True)
        both = jnp.where(lanes == 0, sq, jnp.where(lanes == 1, sk, 0.0))
        both = jnp.concatenate([both, jnp.zeros((G - rows, DH), jnp.float32)], axis=0)
        ssb[y, slot] = both.T[:8, :]
        for h in range(heads):
            vbuf[h, k * NY + slot] = qkv[:, 2 * G + h * DH : 2 * G + (h + 1) * DH].astype(jnp.bfloat16)

    def ss_copies(slot):
        return [
            remote(ssb.at[y, slot], ssb.at[y, slot], ss_send.at[n, slot], ss_recv.at[y, slot], dev)
            for n, dev in enumerate((y2, yp, ym))
        ]

    def kv_copy(which, slot):
        buf = (kbuf, vbuf)[which]
        at = k * NY + slot
        return remote(buf.at[:, at], buf.at[:, at], kv_send.at[which, slot], kv_recv.at[which, at], partner)

    def kv_wait(which, at):
        buf = (kbuf, vbuf)[which]
        pltpu.make_async_copy(buf.at[:, at], buf.at[:, at], kv_recv.at[which, at]).wait()

    position = lax.broadcasted_iota(jnp.int32, (8, 2 * NY * rows), 1)
    bias[...] = jnp.where(position < length[0], 0.0, -1e30)
    for c in loc_w:
        c.wait()
    ring_open(0)
    x_wait(y, 0)
    x_sends[0].start()
    ring_step(0, 0, 1)
    ring_second(0)
    ring_step(0, 0, 2)
    x_wait(y, 1)
    for c in x_sends[1:4]:
        c.start()
    ring_step(0, 1, 1)
    ring_step(0, 0, 3)
    layer_in(y)
    ring_step(0, 1, 2)
    ring_step(0, 0, 4)
    x_wait(below, 0)
    x_sends[4].start()
    x_wait(above, 1)
    x_sends[5].start()
    ring_step(0, 1, 3)
    ring_step(0, 1, 4)
    loc_wo.wait()
    ring_open(1)
    ring_shared(0)

    order = (y, below, above, across)
    for i, slot in enumerate(order):
        if i > 0:
            if i == 1:
                x_wait(below, 1)
            elif i == 2:
                x_wait(above, 0)
            else:
                x_wait(across, 0)
                x_wait(across, 1)
            layer_in(slot)
        project(slot)
        for c in ss_copies(slot):
            c.start()
        kv_copy(1, slot).start()
        if i == 0:
            ring_second(1)
        elif i == 1:
            ring_step(1, 0, 1)
        elif i == 2:
            ring_step(1, 1, 1)

    factor = math.log2(math.e) / math.sqrt(DH)
    cols = pl.ds(pl.multiple_of(y * G, G), G)
    qgain = qg[:, cols] * factor
    kgain = kg[:, cols]

    def finish(slot, which):
        total = ssb[0, slot] + ssb[1, slot] + ssb[2, slot] + ssb[3, slot]
        inv = lax.rsqrt(total * (1.0 / width) + EPS)
        inv = jnp.concatenate([inv, jnp.zeros((DH - 8, G), jnp.float32)], axis=0).T
        q = (qk32[slot, :, :G] * inv[:rows, 0:1] * qgain).astype(jnp.bfloat16)
        kk = (qk32[slot, :, G:] * inv[:rows, 1:2] * kgain).astype(jnp.bfloat16)
        for h in range(heads):
            kbuf[h, k * NY + slot] = kk[:, h * DH : (h + 1) * DH]
            qbuf[slot, h] = q[:, h * DH : (h + 1) * DH]

    for slot in order:
        for src in (below, above, across):
            pltpu.make_async_copy(ssb.at[src, slot], ssb.at[src, slot], ss_recv.at[src, slot]).wait()
        finish(slot, 0)
        kv_copy(0, slot).start()
    ring_step(1, 0, 2)
    ring_step(1, 1, 2)
    for which in (1, 0):
        for slot in range(NY):
            kv_wait(which, (1 - k) * NY + slot)

    keys = 2 * NY * rows

    def attend(slot, h):
        q = qbuf[slot, h]
        sc = lax.dot_general(
            q, kbuf[h].reshape(keys, DH), (((1,), (1,)), ((), ())), preferred_element_type=jnp.float32
        )
        sc = sc + bias[0:1, :]
        top = jnp.max(sc, axis=1, keepdims=True)
        pr = jnp.exp2(sc - top)
        total = jnp.sum(pr, axis=1, keepdims=True)
        o = jnp.dot(pr.astype(jnp.bfloat16), vbuf[h].reshape(keys, DH), preferred_element_type=jnp.float32)
        att_s[slot, h] = (o / total).astype(jnp.bfloat16)

    def at_copy(n, slot, dev):
        return remote(att_s.at[slot], att_r.at[y], at_send.at[n], at_recv.at[y], dev)

    dests = ((across, y2), (above, yp), (below, ym), (y, None))

    for n, (slot, dev) in enumerate(dests):

        def head(h, carry, slot=slot):
            attend(slot, h)
            return carry

        lax.fori_loop(0, heads, head, 0)
        if dev is not None:
            at_copy(n, slot, dev).start()
        if n == 0:
            ring_step(1, 0, 3)
            ring_step(1, 1, 3)
        elif n == 1:
            ring_step(1, 0, 4)
            ring_step(1, 1, 4)

    ring_shared(1)
    per = R // NY if R >= NY else 1

    def out_rows(g):
        if R >= NY:
            return WO[pl.ds(g * per, per)].reshape(G, width)
        return WO[0, pl.ds(pl.multiple_of(g * G, G), G), :]

    def joined(ref, g):
        return jnp.concatenate([ref[g, h] for h in range(heads)], axis=1)

    acc[...] = jnp.dot(joined(att_s, y), out_rows(y), preferred_element_type=jnp.float32)
    for g in (above, below, across):
        pltpu.make_async_copy(att_r.at[g], att_r.at[g], at_recv.at[g]).wait()
        acc[...] += jnp.dot(joined(att_r, g), out_rows(g), preferred_element_type=jnp.float32)

    def tail(i, carry):
        at = pl.ds(pl.multiple_of(i * CH, CH), CH)
        x = X[y, at, :].astype(jnp.float32)
        b = (x + mod[2:3, :] * acc[at, :]).astype(jnp.bfloat16).astype(jnp.float32)
        xn[at, :] = norm_rows(b, mod[4:5, :], mod[3:4, :]).astype(jnp.bfloat16)
        return carry

    lax.fori_loop(0, rows // CH, tail, 0)
    vel = jnp.dot(xn[...], whead[...], preferred_element_type=jnp.float32).astype(jnp.bfloat16)
    C = vel.shape[1] // 2
    vsend[0, :, :C] = vel[:, :C]
    vsend[1, :, :C] = vel[:, C:]

    for c in range(2):
        here = jnp.logical_and(p == k, k == c)

        @pl.when(here)
        def _():
            pltpu.make_async_copy(vsend.at[c], vrecv.at[p], v_recv.at[p]).start()

        @pl.when(jnp.logical_not(here))
        def _():
            remote(vsend.at[c], vrecv.at[p], v_send.at[c], v_recv.at[p], (c, r, k * NY + y)).start()

    for q in range(2):
        pltpu.make_async_copy(vrecv.at[q], vrecv.at[q], v_recv.at[q]).wait()
    cond = vrecv[0, :, :C].astype(jnp.float32)
    uncond = vrecv[1, :, :C].astype(jnp.float32)
    out[...] = uncond + guid[0] * (cond - uncond)

    @pl.when(k != p)
    def _():
        for c in t_copies:
            c.wait_send()

    for c in x_sends:
        c.wait_send()
    for m in range(2):
        ring_drain(m)
    for slot in range(NY):
        for c in ss_copies(slot):
            c.wait_send()
        for which in range(2):
            kv_copy(which, slot).wait_send()
    for n, (slot, dev) in enumerate(dests):
        if dev is not None:
            at_copy(n, slot, dev).wait_send()
    for c in range(2):
        here = jnp.logical_and(p == k, k == c)

        @pl.when(jnp.logical_not(here))
        def _():
            remote(vsend.at[c], vrecv.at[p], v_send.at[c], v_recv.at[p], (c, r, k * NY + y)).wait_send()


def solution(mesh):
    R = mesh.shape["req"]
    NX = 2 if R > 1 else 1
    NZ = R // NX
    DMA = pltpu.SemaphoreType.DMA
    bf, f32 = jnp.bfloat16, jnp.float32

    def local(hidden, latent, modulation, w_qkv, w_out, q_gain, k_gain, w_head, lengths, guidance, step_size):
        rows, width = hidden.shape[2:]
        G = width // NY
        heads = G // DH
        wr = w_qkv.shape[0]
        half = max(NZ // 2, 1)
        chans = w_head.shape[1] // 2
        seq = 2 * NY
        vmem = pl.BlockSpec(memory_space=pltpu.VMEM)
        smem = pl.BlockSpec(memory_space=pltpu.SMEM)
        hbm = pl.BlockSpec(memory_space=pl.ANY)
        guided = pl.pallas_call(
            functools.partial(kernel, NX, NZ),
            out_shape=jax.ShapeDtypeStruct((rows, chans), f32),
            in_specs=[hbm, hbm, hbm, vmem, vmem, vmem, vmem, smem, smem],
            out_specs=vmem,
            scratch_shapes=[
                pltpu.VMEM((NY, rows, width), bf),
                pltpu.VMEM((R, wr, 3 * G), bf),
                pltpu.VMEM((R, wr, width), bf),
                pltpu.VMEM((rows, width), bf),
                pltpu.VMEM((NY, rows, 2 * G), f32),
                pltpu.VMEM((NY, NY, 8, G), f32),
                pltpu.VMEM((NY, heads, rows, DH), bf),
                pltpu.VMEM((heads, seq, rows, DH), bf),
                pltpu.VMEM((heads, seq, rows, DH), bf),
                pltpu.VMEM((NY, heads, rows, DH), bf),
                pltpu.VMEM((NY, heads, rows, DH), bf),
                pltpu.VMEM((rows, width), f32),
                pltpu.VMEM((2, rows, DH), bf),
                pltpu.VMEM((2, rows, DH), bf),
                pltpu.VMEM((8, seq * rows), f32),
                DMA((NY, 2)),
                DMA((2,)),
                DMA((6,)),
                DMA((2, R)),
                DMA((2, 2, half)),
                DMA((2, 2, half)),
                DMA((2,)),
                DMA((4,)),
                DMA((3, NY)),
                DMA((NY, NY)),
                DMA((2, NY)),
                DMA((2, seq)),
                DMA((4,)),
                DMA((NY,)),
                DMA((2,)),
                DMA((2,)),
            ],
            compiler_params=pltpu.CompilerParams(
                collective_id=0, has_side_effects=True, vmem_limit_bytes=60 * 1024 * 1024
            ),
            name="block",
        )(
            hidden[0, 0],
            w_qkv,
            w_out,
            modulation[0],
            q_gain[None],
            k_gain[None],
            w_head,
            lengths,
            guidance,
        )
        position = lax.axis_index("seq")
        valid = position * rows + jnp.arange(rows, dtype=jnp.int32) < lengths[0]
        current = latent[0]
        return jnp.where(valid[:, None], current - step_size[0] * guided, current)[None]

    return jax.shard_map(
        local,
        mesh=mesh,
        in_specs=(
            P("cfg", "req", "seq", None),
            P("req", "seq", "cfg"),
            P("req", None, None),
            P("req", None),
            P("req", None),
            P(),
            P(),
            P(),
            P("req"),
            P("req"),
            P("req"),
        ),
        out_specs=P("req", "seq", "cfg"),
        check_vma=False,
    )
```

```python
import functools
import math

import jax
import jax.numpy as jnp
from jax import lax
from jax.experimental import pallas as pl
from jax.experimental.pallas import tpu as pltpu
from jax.sharding import PartitionSpec as P

MESH = pl.DeviceIdType.MESH
DH = 128
NY = 4
EPS = 1e-6
CH = 48


def norm_rows(x, scale, shift):
    c = x - jnp.mean(x, axis=-1, keepdims=True)
    return c * lax.rsqrt(jnp.mean(c * c, axis=-1, keepdims=True) + EPS) * (1.0 + scale) + shift


def kernel(
    NX,
    NZ,
    hid,
    wqkv,
    wout,
    mod,
    qg,
    kg,
    whead,
    length,
    guid,
    step,
    out,
    X,
    W,
    WO,
    xn,
    qk32,
    ssb,
    qbuf,
    kbuf,
    vbuf,
    att_s,
    att_r,
    acc,
    vsend,
    vrecv,
    bias,
    x_recv,
    t_send,
    y_send,
    w_recv,
    ring_send,
    share_send,
    xe_send,
    loc_sem,
    ss_send,
    ss_recv,
    kv_send,
    kv_recv,
    at_send,
    at_recv,
    v_send,
    v_recv,
):
    rows, width = hid.shape
    G = width // NY
    heads = G // DH
    HR = rows // 2
    R = NX * NZ
    half = NZ // 2
    k = lax.axis_index("cfg")
    r = lax.axis_index("req")
    s = lax.axis_index("seq")
    xh, z = r // NZ, r % NZ
    p, y = s // NY, s % NY

    def seq_of(a, b):
        return a * NY + b % NY

    yp = (k, r, seq_of(p, y + 1))
    ym = (k, r, seq_of(p, y + 3))
    y2 = (k, r, seq_of(p, y + 2))
    transposed = (p, r, k * NY + y)
    partner = (1 - k, r, s)
    xpart = (k, (1 - xh) * NZ + z, s)
    znext = (k, xh * NZ + (z + 1 + k * (NZ - 2)) % NZ, s)

    def remote(src, dst, ssem, rsem, dev):
        return pltpu.make_async_remote_copy(
            src_ref=src, dst_ref=dst, send_sem=ssem, recv_sem=rsem, device_id=dev, device_id_type=MESH
        )

    barrier = pltpu.get_barrier_semaphore()
    peers = [
        yp,
        ym,
        y2,
        partner,
        (k, r, (1 - p) * NY + y),
        (1 - k, r, (1 - p) * NY + y),
    ]
    if NX > 1:
        peers.append(xpart)
    if NZ > 1:
        peers.append((k, xh * NZ + (z + 1) % NZ, s))
        peers.append((k, xh * NZ + (z + NZ - 1) % NZ, s))
    for dev in peers:
        pl.semaphore_signal(barrier, inc=1, device_id=dev, device_id_type=MESH)
    loc_w = [
        pltpu.make_async_copy(
            wqkv.at[:, pl.ds(pl.multiple_of(j * width + y * G, G), G)],
            W.at[r, :, pl.ds(j * G, G)],
            loc_sem.at[j],
        )
        for j in range(3)
    ]
    loc_wo = pltpu.make_async_copy(wout, WO.at[r], loc_sem.at[3])
    for c in loc_w:
        c.start()
    loc_wo.start()

    def hrows(h):
        return pl.ds(h * HR, HR)

    @pl.when(k == p)
    def _():
        for h in range(2):
            pltpu.make_async_copy(hid.at[hrows(h)], X.at[y, hrows(h)], x_recv.at[y, h]).start()

    pl.semaphore_wait(barrier, len(peers))

    t_copies = [
        remote(hid.at[hrows(h)], X.at[y, hrows(h)], t_send.at[h], x_recv.at[y, h], transposed) for h in range(2)
    ]

    @pl.when(k != p)
    def _():
        for c in t_copies:
            c.start()

    bufs = (W, WO)

    def slot_at(side, t):
        other = xh if side == 0 else 1 - xh
        return other * NZ + (z + t * (NZ - 1) + k * 2 * t) % NZ

    def ring_copy(m, side, t):
        j = slot_at(side, t)
        return remote(bufs[m].at[j], bufs[m].at[j], ring_send.at[m, side, t], w_recv.at[m, j], znext)

    def share_copy(m, side, t):
        j = slot_at(side, t)
        return remote(bufs[m].at[j], bufs[m].at[j], share_send.at[m, side, t - 1], w_recv.at[m, j], partner)

    def mine(side):
        return (xh if side == 0 else 1 - xh) == k

    def recv_wait(m, j):
        pltpu.make_async_copy(bufs[m].at[j], bufs[m].at[j], w_recv.at[m, j]).wait()

    def ring_start(m, side):
        if NZ > 1:
            if half > 1:
                ring_copy(m, side, 0).start()
            else:

                @pl.when(mine(side))
                def _():
                    ring_copy(m, side, 0).start()

    def xe_copy(m):
        return remote(bufs[m].at[r], bufs[m].at[r], xe_send.at[m], w_recv.at[m, r], xpart)

    def xe_start(m):
        if NX > 1:

            @pl.when(k == m)
            def _():
                xe_copy(m).start()

    def xe_share(m):
        j = slot_at(1, 0)
        return remote(bufs[m].at[j], bufs[m].at[j], xe_send.at[2 + m], w_recv.at[m, j], partner)

    def ring_second(m):
        if NX > 1:
            recv_wait(m, slot_at(1, 0))
            ring_start(m, 1)

            @pl.when(k == m)
            def _():
                xe_share(m).start()

    def ring_step(m, side, t):
        if NZ == 1 or t > half or side >= NX:
            return

        def go():
            recv_wait(m, slot_at(side, t))
            if t < half - 1:
                ring_copy(m, side, t).start()
            elif t == half - 1:

                @pl.when(mine(side))
                def _():
                    ring_copy(m, side, t).start()

            share_copy(m, side, t).start()

        if t < half:
            go()
        else:
            pl.when(mine(side))(go)

    def ring_shared(m):
        for side in range(NX):
            for t in range(half + 1, NZ):
                recv_wait(m, slot_at(side, t))
            if NZ > 1:

                @pl.when(jnp.logical_not(mine(side)))
                def _():
                    recv_wait(m, slot_at(side, half))

    def ring_drain(m):
        if NX > 1:

            @pl.when(k == m)
            def _():
                xe_copy(m).wait_send()
                xe_share(m).wait_send()

        for side in range(NX):
            for t in range(half):
                if t < half - 1:
                    ring_copy(m, side, t).wait_send()
                else:

                    @pl.when(mine(side))
                    def _():
                        ring_copy(m, side, t).wait_send()

            for t in range(1, half + 1):
                if t < half:
                    share_copy(m, side, t).wait_send()
                else:

                    @pl.when(mine(side))
                    def _():
                        share_copy(m, side, t).wait_send()

    def x_copy(slot, h, n, dev):
        return remote(X.at[slot, hrows(h)], X.at[slot, hrows(h)], y_send.at[n], x_recv.at[slot, h], dev)

    def x_wait(slot, h):
        pltpu.make_async_copy(X.at[slot, hrows(h)], X.at[slot, hrows(h)], x_recv.at[slot, h]).wait()

    below, above, across = (y + 3) % NY, (y + 1) % NY, (y + 2) % NY
    x_sends = [
        x_copy(y, 0, 0, yp),
        x_copy(y, 0, 1, ym),
        x_copy(y, 1, 2, ym),
        x_copy(y, 1, 3, yp),
        x_copy(below, 0, 4, yp),
        x_copy(above, 1, 5, ym),
    ]

    def layer_in(slot):
        def chunk(i, carry):
            at = pl.ds(pl.multiple_of(i * CH, CH), CH)
            x = X[slot, at, :].astype(jnp.float32)
            xn[at, :] = norm_rows(x, mod[1], mod[0]).astype(jnp.bfloat16)
            return carry

        lax.fori_loop(0, rows // CH, chunk, 0)

    lanes = lax.broadcasted_iota(jnp.int32, (rows, DH), 1)

    def project(slot):
        qkv = jnp.dot(xn[...], W[...].reshape(width, 3 * G), preferred_element_type=jnp.float32)
        q = qkv[:, :G]
        kk = qkv[:, G : 2 * G]
        qk32[slot] = qkv[:, : 2 * G]
        sq = jnp.sum(q * q, axis=1, keepdims=True)
        sk = jnp.sum(kk * kk, axis=1, keepdims=True)
        both = jnp.where(lanes == 0, sq, jnp.where(lanes == 1, sk, 0.0))
        both = jnp.concatenate([both, jnp.zeros((G - rows, DH), jnp.float32)], axis=0)
        ssb[y, slot] = both.T[:8, :]
        for h in range(heads):
            vbuf[h, k * NY + slot] = qkv[:, 2 * G + h * DH : 2 * G + (h + 1) * DH].astype(jnp.bfloat16)

    def ss_copies(slot):
        return [
            remote(ssb.at[y, slot], ssb.at[y, slot], ss_send.at[n, slot], ss_recv.at[y, slot], dev)
            for n, dev in enumerate((y2, yp, ym))
        ]

    def kv_copy(which, slot):
        buf = (kbuf, vbuf)[which]
        at = k * NY + slot
        return remote(buf.at[:, at], buf.at[:, at], kv_send.at[which, slot], kv_recv.at[which, at], partner)

    def kv_wait(which, at):
        buf = (kbuf, vbuf)[which]
        pltpu.make_async_copy(buf.at[:, at], buf.at[:, at], kv_recv.at[which, at]).wait()

    early = k == p

    def when_early(*steps):
        @pl.when(early)
        def _():
            for step in steps:
                step()

    def when_late(*steps):
        @pl.when(jnp.logical_not(early))
        def _():
            for step in steps:
                step()

    def own_half(h):
        x_wait(y, h)
        x_sends[2 * h].start()
        x_sends[2 * h + 1].start()

    def pass_below():
        x_wait(below, 0)
        x_sends[4].start()

    def pass_above():
        x_wait(above, 1)
        x_sends[5].start()

    for c in loc_w:
        c.wait()
    ring_start(0, 0)
    xe_start(0)
    when_early(lambda: own_half(0), lambda: own_half(1), lambda: layer_in(y))
    position = lax.broadcasted_iota(jnp.int32, (8, 2 * NY * rows), 1)
    bias[...] = jnp.where(position < length[0], 0.0, -1e30)
    ring_step(0, 0, 1)
    ring_second(0)
    when_late(lambda: own_half(0))
    ring_step(0, 0, 2)
    when_early(pass_below)
    ring_step(0, 1, 1)
    when_early(pass_above)
    when_late(lambda: own_half(1))
    loc_wo.wait()
    xe_start(1)
    ring_step(0, 0, 3)
    when_late(lambda: layer_in(y))
    ring_step(0, 1, 2)
    when_late(pass_below, pass_above)
    ring_step(0, 0, 4)
    ring_step(0, 1, 3)
    ring_start(1, 0)
    ring_step(0, 1, 4)
    ring_second(1)
    ring_shared(0)

    order = (y, below, above, across)
    for i, slot in enumerate(order):
        if i > 0:
            if i == 1:
                x_wait(below, 1)
            elif i == 2:
                x_wait(above, 0)
            else:
                x_wait(across, 0)
                x_wait(across, 1)
            layer_in(slot)
        project(slot)
        for c in ss_copies(slot):
            c.start()
        kv_copy(1, slot).start()
        if i == 0:
            ring_step(1, 0, 1)
        elif i == 1:
            ring_step(1, 1, 1)
        elif i == 2:
            ring_step(1, 0, 2)
        else:
            ring_step(1, 1, 2)

    factor = math.log2(math.e) / math.sqrt(DH)
    cols = pl.ds(pl.multiple_of(y * G, G), G)
    qgain = qg[cols].reshape(1, G) * factor
    kgain = kg[cols].reshape(1, G)

    def finish(slot, which):
        total = ssb[0, slot] + ssb[1, slot] + ssb[2, slot] + ssb[3, slot]
        inv = lax.rsqrt(total * (1.0 / width) + EPS)
        inv = jnp.concatenate([inv, jnp.zeros((DH - 8, G), jnp.float32)], axis=0).T
        q = (qk32[slot, :, :G] * inv[:rows, 0:1] * qgain).astype(jnp.bfloat16)
        kk = (qk32[slot, :, G:] * inv[:rows, 1:2] * kgain).astype(jnp.bfloat16)
        for h in range(heads):
            kbuf[h, k * NY + slot] = kk[:, h * DH : (h + 1) * DH]
            qbuf[slot, h] = q[:, h * DH : (h + 1) * DH]

    for slot in order:
        for src in (below, above, across):
            pltpu.make_async_copy(ssb.at[src, slot], ssb.at[src, slot], ss_recv.at[src, slot]).wait()
        finish(slot, 0)
        kv_copy(0, slot).start()
    ring_step(1, 0, 3)
    ring_step(1, 1, 3)
    for which in (1, 0):
        for slot in range(NY):
            kv_wait(which, (1 - k) * NY + slot)

    keys = 2 * NY * rows

    def attend(slot, h):
        q = qbuf[slot, h]
        sc = lax.dot_general(
            q, kbuf[h].reshape(keys, DH), (((1,), (1,)), ((), ())), preferred_element_type=jnp.float32
        )
        sc = sc + bias[0:1, :]
        top = jnp.max(sc, axis=1, keepdims=True)
        pr = jnp.exp2(sc - top)
        total = jnp.sum(pr, axis=1, keepdims=True)
        o = jnp.dot(pr.astype(jnp.bfloat16), vbuf[h].reshape(keys, DH), preferred_element_type=jnp.float32)
        att_s[slot, h] = (o / total).astype(jnp.bfloat16)

    def at_copy(n, slot, dev):
        return remote(att_s.at[slot], att_r.at[y], at_send.at[n], at_recv.at[y], dev)

    dests = ((across, y2), (above, yp), (below, ym), (y, None))

    for n, (slot, dev) in enumerate(dests):

        def head(h, carry, slot=slot):
            attend(slot, h)
            return carry

        lax.fori_loop(0, heads, head, 0, unroll=True)
        if dev is not None:
            at_copy(n, slot, dev).start()
        if n == 0:
            ring_step(1, 0, 4)
        elif n == 1:
            ring_step(1, 1, 4)

    ring_shared(1)
    per = R // NY if R >= NY else 1

    def out_rows(g):
        if R >= NY:
            return WO[pl.ds(g * per, per)].reshape(G, width)
        return WO[0, pl.ds(pl.multiple_of(g * G, G), G), :]

    def joined(ref, g):
        return jnp.concatenate([ref[g, h] for h in range(heads)], axis=1)

    acc[...] = jnp.dot(joined(att_s, y), out_rows(y), preferred_element_type=jnp.float32)
    for g in (above, below, across):
        pltpu.make_async_copy(att_r.at[g], att_r.at[g], at_recv.at[g]).wait()
        acc[...] += jnp.dot(joined(att_r, g), out_rows(g), preferred_element_type=jnp.float32)

    def tail(i, carry):
        at = pl.ds(pl.multiple_of(i * CH, CH), CH)
        x = X[y, at, :].astype(jnp.float32)
        b = (x + mod[2] * acc[at, :]).astype(jnp.bfloat16).astype(jnp.float32)
        xn[at, :] = norm_rows(b, mod[4], mod[3]).astype(jnp.bfloat16)
        return carry

    lax.fori_loop(0, rows // CH, tail, 0)
    vel = lax.dot_general(whead[...], xn[...], (((1,), (1,)), ((), ())), preferred_element_type=jnp.float32)
    C = vel.shape[0] // 2
    for c in range(2):
        vsend[c, :, :rows] = vel[c * C : (c + 1) * C].astype(jnp.bfloat16)

    for c in range(2):
        here = jnp.logical_and(p == k, k == c)

        @pl.when(here)
        def _():
            pltpu.make_async_copy(vsend.at[c], vrecv.at[p], v_recv.at[p]).start()

        @pl.when(jnp.logical_not(here))
        def _():
            remote(vsend.at[c], vrecv.at[p], v_send.at[c], v_recv.at[p], (c, r, k * NY + y)).start()

    for q in range(2):
        pltpu.make_async_copy(vrecv.at[q], vrecv.at[q], v_recv.at[q]).wait()
    cond = vrecv[0, :, :rows].astype(jnp.float32)
    uncond = vrecv[1, :, :rows].astype(jnp.float32)
    token = s * rows + lax.broadcasted_iota(jnp.int32, out.shape, 1)
    out[...] = jnp.where(token < length[0], step[0] * (uncond + guid[0] * (cond - uncond)), 0.0)

    @pl.when(k != p)
    def _():
        for c in t_copies:
            c.wait_send()

    for c in x_sends:
        c.wait_send()
    for m in range(2):
        ring_drain(m)
    for slot in range(NY):
        for c in ss_copies(slot):
            c.wait_send()
        for which in range(2):
            kv_copy(which, slot).wait_send()
    for n, (slot, dev) in enumerate(dests):
        if dev is not None:
            at_copy(n, slot, dev).wait_send()
    for c in range(2):
        here = jnp.logical_and(p == k, k == c)

        @pl.when(jnp.logical_not(here))
        def _():
            remote(vsend.at[c], vrecv.at[p], v_send.at[c], v_recv.at[p], (c, r, k * NY + y)).wait_send()


def solution(mesh):
    R = mesh.shape["req"]
    NX = 2 if R > 1 else 1
    NZ = R // NX
    DMA = pltpu.SemaphoreType.DMA
    bf, f32 = jnp.bfloat16, jnp.float32

    def local(hidden, latent, modulation, w_qkv, w_out, q_gain, k_gain, w_head, lengths, guidance, step_size):
        rows, width = hidden.shape[2:]
        G = width // NY
        heads = G // DH
        wr = w_qkv.shape[0]
        half = max(NZ // 2, 1)
        chans = w_head.shape[1] // 2
        seq = 2 * NY
        vmem = pl.BlockSpec(memory_space=pltpu.VMEM)
        smem = pl.BlockSpec(memory_space=pltpu.SMEM)
        hbm = pl.BlockSpec(memory_space=pl.ANY)
        change = pl.pallas_call(
            functools.partial(kernel, NX, NZ),
            out_shape=jax.ShapeDtypeStruct((chans, rows), f32),
            in_specs=[hbm, hbm, hbm, vmem, vmem, vmem, vmem, smem, smem, smem],
            out_specs=vmem,
            scratch_shapes=[
                pltpu.VMEM((NY, rows, width), bf),
                pltpu.VMEM((R, wr, 3 * G), bf),
                pltpu.VMEM((R, wr, width), bf),
                pltpu.VMEM((rows, width), bf),
                pltpu.VMEM((NY, rows, 2 * G), f32),
                pltpu.VMEM((NY, NY, 8, G), f32),
                pltpu.VMEM((NY, heads, rows, DH), bf),
                pltpu.VMEM((heads, seq, rows, DH), bf),
                pltpu.VMEM((heads, seq, rows, DH), bf),
                pltpu.VMEM((NY, heads, rows, DH), bf),
                pltpu.VMEM((NY, heads, rows, DH), bf),
                pltpu.VMEM((rows, width), f32),
                pltpu.VMEM((2, chans, G), bf),
                pltpu.VMEM((2, chans, G), bf),
                pltpu.VMEM((8, seq * rows), f32),
                DMA((NY, 2)),
                DMA((2,)),
                DMA((6,)),
                DMA((2, R)),
                DMA((2, 2, half)),
                DMA((2, 2, half)),
                DMA((4,)),
                DMA((4,)),
                DMA((3, NY)),
                DMA((NY, NY)),
                DMA((2, NY)),
                DMA((2, seq)),
                DMA((4,)),
                DMA((NY,)),
                DMA((2,)),
                DMA((2,)),
            ],
            compiler_params=pltpu.CompilerParams(
                collective_id=0, has_side_effects=True, vmem_limit_bytes=60 * 1024 * 1024
            ),
            name="block",
        )(
            hidden[0, 0],
            w_qkv,
            w_out,
            jnp.transpose(modulation, (1, 0, 2)),
            q_gain,
            k_gain,
            w_head.T,
            lengths,
            guidance,
            step_size,
        )
        return (latent[0].T - change).T[None]

    return jax.shard_map(
        local,
        mesh=mesh,
        in_specs=(
            P("cfg", "req", "seq", None),
            P("req", "seq", "cfg"),
            P("req", None, None),
            P("req", None),
            P("req", None),
            P(),
            P(),
            P(),
            P("req"),
            P("req"),
            P("req"),
        ),
        out_specs=P("req", "seq", "cfg"),
        check_vma=False,
    )
```

```python
import functools
import math

import jax
import jax.numpy as jnp
from jax import lax
from jax.experimental import pallas as pl
from jax.experimental.pallas import tpu as pltpu
from jax.sharding import PartitionSpec as P

MESH = pl.DeviceIdType.MESH
DH = 128
NY = 4
EPS = 1e-6
CH = 48


def norm_rows(x, scale, shift):
    c = x - jnp.mean(x, axis=-1, keepdims=True)
    return c * lax.rsqrt(jnp.mean(c * c, axis=-1, keepdims=True) + EPS) * (1.0 + scale) + shift


def kernel(
    NX,
    NZ,
    hid,
    wqkv,
    wout,
    mod,
    qg,
    kg,
    whead,
    length,
    guid,
    step,
    out,
    X,
    W,
    WO,
    xn,
    qk32,
    ssb,
    qbuf,
    kbuf,
    vbuf,
    att_s,
    att_r,
    acc,
    vsend,
    vrecv,
    bias,
    x_recv,
    t_send,
    y_send,
    w_recv,
    ring_send,
    share_send,
    xe_send,
    loc_sem,
    ss_send,
    ss_recv,
    kv_send,
    kv_recv,
    at_send,
    at_recv,
    v_send,
    v_recv,
):
    rows, width = hid.shape
    G = width // NY
    heads = G // DH
    HR = rows // 2
    R = NX * NZ
    half = NZ // 2
    k = lax.axis_index("cfg")
    r = lax.axis_index("req")
    s = lax.axis_index("seq")
    xh, z = r // NZ, r % NZ
    p, y = s // NY, s % NY

    def seq_of(a, b):
        return a * NY + b % NY

    yp = (k, r, seq_of(p, y + 1))
    ym = (k, r, seq_of(p, y + 3))
    y2 = (k, r, seq_of(p, y + 2))
    transposed = (p, r, k * NY + y)
    partner = (1 - k, r, s)
    xpart = (k, (1 - xh) * NZ + z, s)
    znext = ((k, xh * NZ + (z + 1) % NZ, s), (k, xh * NZ + (z + NZ - 1) % NZ, s))

    def remote(src, dst, ssem, rsem, dev):
        return pltpu.make_async_remote_copy(
            src_ref=src, dst_ref=dst, send_sem=ssem, recv_sem=rsem, device_id=dev, device_id_type=MESH
        )

    barrier = pltpu.get_barrier_semaphore()
    peers = [
        yp,
        ym,
        y2,
        partner,
        (k, r, (1 - p) * NY + y),
        (1 - k, r, (1 - p) * NY + y),
    ]
    if NX > 1:
        peers.append(xpart)
    if NZ > 1:
        peers.append((k, xh * NZ + (z + 1) % NZ, s))
        peers.append((k, xh * NZ + (z + NZ - 1) % NZ, s))
    for dev in peers:
        pl.semaphore_signal(barrier, inc=1, device_id=dev, device_id_type=MESH)
    loc_w = [
        pltpu.make_async_copy(
            wqkv.at[:, pl.ds(pl.multiple_of(j * width + y * G, G), G)],
            W.at[r, :, pl.ds(j * G, G)],
            loc_sem.at[j],
        )
        for j in range(3)
    ]
    loc_wo = pltpu.make_async_copy(wout, WO.at[r], loc_sem.at[3])
    for c in loc_w:
        c.start()
    loc_wo.start()

    def hrows(h):
        return pl.ds(h * HR, HR)

    @pl.when(k == p)
    def _():
        for h in range(2):
            pltpu.make_async_copy(hid.at[hrows(h)], X.at[y, hrows(h)], x_recv.at[y, h]).start()

    pl.semaphore_wait(barrier, len(peers))

    t_copies = [
        remote(hid.at[hrows(h)], X.at[y, hrows(h)], t_send.at[h], x_recv.at[y, h], transposed) for h in range(2)
    ]

    @pl.when(k != p)
    def _():
        for c in t_copies:
            c.start()

    bufs = (W, WO)

    def slot_at(way, side, t):
        other = xh if side == 0 else 1 - xh
        return other * NZ + (z + (t if way else t * (NZ - 1))) % NZ

    def ring_copy(m, way, side, t):
        j = slot_at(way, side, t)
        return remote(bufs[m].at[j], bufs[m].at[j], ring_send.at[m, way, side, t], w_recv.at[m, j], znext[way])

    def share_copy(m, way, side, t):
        j = slot_at(way, side, t)
        return remote(bufs[m].at[j], bufs[m].at[j], share_send.at[m, way, side, t - 1], w_recv.at[m, j], partner)

    def farthest(way, side):
        return (xh if side == 0 else 1 - xh) == way

    def recv_wait(m, j):
        pltpu.make_async_copy(bufs[m].at[j], bufs[m].at[j], w_recv.at[m, j]).wait()

    def ring_start(m, side):
        for way in range(2 if NZ > 1 else 0):
            ring_copy(m, way, side, 0).start()

    def xe_copy(m):
        return remote(bufs[m].at[r], bufs[m].at[r], xe_send.at[m], w_recv.at[m, r], xpart)

    def xe_share(m):
        j = slot_at(0, 1, 0)
        return remote(bufs[m].at[j], bufs[m].at[j], xe_send.at[2 + m], w_recv.at[m, j], partner)

    def xe_start(m):
        if NX > 1:
            xe_copy(m).start()

    def ring_second(m):
        if NX > 1:
            recv_wait(m, slot_at(0, 1, 0))
            ring_start(m, 1)
            xe_share(m).start()

    def ring_step(m, side, t):
        if NZ == 1:
            return
        for way in range(2):

            def go(way=way):
                recv_wait(m, slot_at(way, side, t))
                if t < half - 1:
                    ring_copy(m, way, side, t).start()
                elif t == half - 1:

                    @pl.when(farthest(way, side))
                    def _():
                        ring_copy(m, way, side, t).start()

                share_copy(m, way, side, t).start()

            if t < half:
                go()
            else:
                pl.when(farthest(way, side))(go)

    def ring_shared(m):
        for side in range(NX):
            for t in range(NZ):
                if side or t:
                    recv_wait(m, slot_at(1, side, t))

    def ring_drain(m):
        if NX > 1:
            xe_copy(m).wait_send()
            xe_share(m).wait_send()
        for way in range(2 if NZ > 1 else 0):
            for side in range(NX):
                for t in range(half - 1):
                    ring_copy(m, way, side, t).wait_send()
                for t in range(1, half):
                    share_copy(m, way, side, t).wait_send()

                @pl.when(farthest(way, side))
                def _():
                    ring_copy(m, way, side, half - 1).wait_send()
                    share_copy(m, way, side, half).wait_send()

    def x_copy(slot, h, n, dev):
        return remote(X.at[slot, hrows(h)], X.at[slot, hrows(h)], y_send.at[n], x_recv.at[slot, h], dev)

    def x_wait(slot, h):
        pltpu.make_async_copy(X.at[slot, hrows(h)], X.at[slot, hrows(h)], x_recv.at[slot, h]).wait()

    below, above, across = (y + 3) % NY, (y + 1) % NY, (y + 2) % NY
    x_sends = [
        x_copy(y, 0, 0, yp),
        x_copy(y, 0, 1, ym),
        x_copy(y, 1, 2, ym),
        x_copy(y, 1, 3, yp),
        x_copy(below, 0, 4, yp),
        x_copy(above, 1, 5, ym),
    ]

    def layer_in(slot):
        def chunk(i, carry):
            at = pl.ds(pl.multiple_of(i * CH, CH), CH)
            x = X[slot, at, :].astype(jnp.float32)
            xn[at, :] = norm_rows(x, mod[1], mod[0]).astype(jnp.bfloat16)
            return carry

        lax.fori_loop(0, rows // CH, chunk, 0)

    lanes = lax.broadcasted_iota(jnp.int32, (rows, DH), 1)

    def project(slot):
        qkv = jnp.dot(xn[...], W[...].reshape(width, 3 * G), preferred_element_type=jnp.float32)
        q = qkv[:, :G]
        kk = qkv[:, G : 2 * G]
        qk32[slot] = qkv[:, : 2 * G]
        sq = jnp.sum(q * q, axis=1, keepdims=True)
        sk = jnp.sum(kk * kk, axis=1, keepdims=True)
        both = jnp.where(lanes == 0, sq, jnp.where(lanes == 1, sk, 0.0))
        both = jnp.concatenate([both, jnp.zeros((G - rows, DH), jnp.float32)], axis=0)
        ssb[y, slot] = both.T[:8, :]
        for h in range(heads):
            vbuf[h, k * NY + slot] = qkv[:, 2 * G + h * DH : 2 * G + (h + 1) * DH].astype(jnp.bfloat16)

    def ss_copies(slot):
        return [
            remote(ssb.at[y, slot], ssb.at[y, slot], ss_send.at[n, slot], ss_recv.at[y, slot], dev)
            for n, dev in enumerate((y2, yp, ym))
        ]

    def kv_copy(which, slot):
        buf = (kbuf, vbuf)[which]
        at = k * NY + slot
        return remote(buf.at[:, at], buf.at[:, at], kv_send.at[which, slot], kv_recv.at[which, at], partner)

    def kv_wait(which, at):
        buf = (kbuf, vbuf)[which]
        pltpu.make_async_copy(buf.at[:, at], buf.at[:, at], kv_recv.at[which, at]).wait()

    early = k == p

    def when_early(*steps):
        @pl.when(early)
        def _():
            for step in steps:
                step()

    def when_late(*steps):
        @pl.when(jnp.logical_not(early))
        def _():
            for step in steps:
                step()

    def own_half(h):
        x_wait(y, h)
        x_sends[2 * h].start()
        x_sends[2 * h + 1].start()

    def pass_below():
        x_wait(below, 0)
        x_sends[4].start()

    def pass_above():
        x_wait(above, 1)
        x_sends[5].start()

    for c in loc_w:
        c.wait()
    when_early(
        lambda: ring_start(0, 0),
        lambda: xe_start(0),
        lambda: own_half(0),
        lambda: own_half(1),
        lambda: layer_in(y),
    )
    position = lax.broadcasted_iota(jnp.int32, (8, 2 * NY * rows), 1)
    bias[...] = jnp.where(position < length[0], 0.0, -1e30)
    loc_wo.wait()
    when_early(
        lambda: ring_step(0, 0, 1),
        lambda: ring_second(0),
        lambda: ring_step(0, 0, 2),
        pass_below,
        lambda: ring_step(0, 1, 1),
        pass_above,
        lambda: ring_step(0, 0, 3),
        lambda: ring_step(0, 1, 2),
        lambda: ring_step(0, 0, 4),
        lambda: ring_step(0, 1, 3),
        lambda: ring_step(0, 1, 4),
    )
    when_late(
        lambda: own_half(0),
        lambda: own_half(1),
        lambda: xe_start(1),
        lambda: layer_in(y),
        lambda: ring_start(1, 0),
        pass_below,
        pass_above,
        lambda: ring_second(1),
        lambda: ring_step(1, 0, 1),
        lambda: ring_shared(0),
    )

    order = (y, below, above, across)
    for i, slot in enumerate(order):
        if i > 0:
            if i == 1:
                x_wait(below, 1)
            elif i == 2:
                x_wait(above, 0)
            else:
                x_wait(across, 0)
                x_wait(across, 1)
            layer_in(slot)
        project(slot)
        for c in ss_copies(slot):
            c.start()
        kv_copy(1, slot).start()
        side, t = ((1, 1), (0, 2), (1, 2), (0, 3))[i]
        when_late(lambda: ring_step(1, side, t))

    factor = math.log2(math.e) / math.sqrt(DH)
    cols = pl.ds(pl.multiple_of(y * G, G), G)
    qgain = qg[cols].reshape(1, G) * factor
    kgain = kg[cols].reshape(1, G)

    def finish(slot, which):
        total = ssb[0, slot] + ssb[1, slot] + ssb[2, slot] + ssb[3, slot]
        inv = lax.rsqrt(total * (1.0 / width) + EPS)
        inv = jnp.concatenate([inv, jnp.zeros((DH - 8, G), jnp.float32)], axis=0).T
        q = (qk32[slot, :, :G] * inv[:rows, 0:1] * qgain).astype(jnp.bfloat16)
        kk = (qk32[slot, :, G:] * inv[:rows, 1:2] * kgain).astype(jnp.bfloat16)
        for h in range(heads):
            kbuf[h, k * NY + slot] = kk[:, h * DH : (h + 1) * DH]
            qbuf[slot, h] = q[:, h * DH : (h + 1) * DH]

    for slot in order:
        for src in (below, above, across):
            pltpu.make_async_copy(ssb.at[src, slot], ssb.at[src, slot], ss_recv.at[src, slot]).wait()
        finish(slot, 0)
        kv_copy(0, slot).start()
    when_late(lambda: ring_step(1, 1, 3))
    for which in (1, 0):
        for slot in range(NY):
            kv_wait(which, (1 - k) * NY + slot)

    keys = 2 * NY * rows

    def attend(slot, h):
        q = qbuf[slot, h]
        sc = lax.dot_general(
            q, kbuf[h].reshape(keys, DH), (((1,), (1,)), ((), ())), preferred_element_type=jnp.float32
        )
        sc = sc + bias[0:1, :]
        top = jnp.max(sc, axis=1, keepdims=True)
        pr = jnp.exp2(sc - top)
        total = jnp.sum(pr, axis=1, keepdims=True)
        o = jnp.dot(pr.astype(jnp.bfloat16), vbuf[h].reshape(keys, DH), preferred_element_type=jnp.float32)
        att_s[slot, h] = (o / total).astype(jnp.bfloat16)

    def at_copy(n, slot, dev):
        return remote(att_s.at[slot], att_r.at[y], at_send.at[n], at_recv.at[y], dev)

    dests = ((across, y2), (above, yp), (below, ym), (y, None))

    for n, (slot, dev) in enumerate(dests):

        def head(h, carry, slot=slot):
            attend(slot, h)
            return carry

        lax.fori_loop(0, heads, head, 0, unroll=True)
        if dev is not None:
            at_copy(n, slot, dev).start()
        if n < 2:
            when_late(lambda: ring_step(1, n, 4))

    when_early(lambda: ring_shared(1))
    per = R // NY if R >= NY else 1

    def out_rows(g):
        if R >= NY:
            return WO[pl.ds(g * per, per)].reshape(G, width)
        return WO[0, pl.ds(pl.multiple_of(g * G, G), G), :]

    def joined(ref, g):
        return jnp.concatenate([ref[g, h] for h in range(heads)], axis=1)

    acc[...] = jnp.dot(joined(att_s, y), out_rows(y), preferred_element_type=jnp.float32)
    for g in (above, below, across):
        pltpu.make_async_copy(att_r.at[g], att_r.at[g], at_recv.at[g]).wait()
        acc[...] += jnp.dot(joined(att_r, g), out_rows(g), preferred_element_type=jnp.float32)

    def tail(i, carry):
        at = pl.ds(pl.multiple_of(i * CH, CH), CH)
        x = X[y, at, :].astype(jnp.float32)
        b = (x + mod[2] * acc[at, :]).astype(jnp.bfloat16).astype(jnp.float32)
        xn[at, :] = norm_rows(b, mod[4], mod[3]).astype(jnp.bfloat16)
        return carry

    lax.fori_loop(0, rows // CH, tail, 0)
    vel = lax.dot_general(whead[...], xn[...], (((1,), (1,)), ((), ())), preferred_element_type=jnp.float32)
    C = vel.shape[0] // 2
    for c in range(2):
        vsend[c, :, :rows] = vel[c * C : (c + 1) * C].astype(jnp.bfloat16)

    for c in range(2):
        here = jnp.logical_and(p == k, k == c)

        @pl.when(here)
        def _():
            pltpu.make_async_copy(vsend.at[c], vrecv.at[p], v_recv.at[p]).start()

        @pl.when(jnp.logical_not(here))
        def _():
            remote(vsend.at[c], vrecv.at[p], v_send.at[c], v_recv.at[p], (c, r, k * NY + y)).start()

    for q in range(2):
        pltpu.make_async_copy(vrecv.at[q], vrecv.at[q], v_recv.at[q]).wait()
    cond = vrecv[0, :, :rows].astype(jnp.float32)
    uncond = vrecv[1, :, :rows].astype(jnp.float32)
    token = s * rows + lax.broadcasted_iota(jnp.int32, out.shape, 1)
    out[...] = jnp.where(token < length[0], step[0] * (uncond + guid[0] * (cond - uncond)), 0.0)

    @pl.when(k != p)
    def _():
        for c in t_copies:
            c.wait_send()

    for c in x_sends:
        c.wait_send()
    when_early(lambda: ring_drain(0))
    when_late(lambda: ring_drain(1))
    for slot in range(NY):
        for c in ss_copies(slot):
            c.wait_send()
        for which in range(2):
            kv_copy(which, slot).wait_send()
    for n, (slot, dev) in enumerate(dests):
        if dev is not None:
            at_copy(n, slot, dev).wait_send()
    for c in range(2):
        here = jnp.logical_and(p == k, k == c)

        @pl.when(jnp.logical_not(here))
        def _():
            remote(vsend.at[c], vrecv.at[p], v_send.at[c], v_recv.at[p], (c, r, k * NY + y)).wait_send()


def solution(mesh):
    R = mesh.shape["req"]
    NX = 2 if R > 1 else 1
    NZ = R // NX
    DMA = pltpu.SemaphoreType.DMA
    bf, f32 = jnp.bfloat16, jnp.float32

    def local(hidden, latent, modulation, w_qkv, w_out, q_gain, k_gain, w_head, lengths, guidance, step_size):
        rows, width = hidden.shape[2:]
        G = width // NY
        heads = G // DH
        wr = w_qkv.shape[0]
        half = max(NZ // 2, 1)
        chans = w_head.shape[1] // 2
        seq = 2 * NY
        vmem = pl.BlockSpec(memory_space=pltpu.VMEM)
        smem = pl.BlockSpec(memory_space=pltpu.SMEM)
        hbm = pl.BlockSpec(memory_space=pl.ANY)
        change = pl.pallas_call(
            functools.partial(kernel, NX, NZ),
            out_shape=jax.ShapeDtypeStruct((chans, rows), f32),
            in_specs=[hbm, hbm, hbm, vmem, vmem, vmem, vmem, smem, smem, smem],
            out_specs=vmem,
            scratch_shapes=[
                pltpu.VMEM((NY, rows, width), bf),
                pltpu.VMEM((R, wr, 3 * G), bf),
                pltpu.VMEM((R, wr, width), bf),
                pltpu.VMEM((rows, width), bf),
                pltpu.VMEM((NY, rows, 2 * G), f32),
                pltpu.VMEM((NY, NY, 8, G), f32),
                pltpu.VMEM((NY, heads, rows, DH), bf),
                pltpu.VMEM((heads, seq, rows, DH), bf),
                pltpu.VMEM((heads, seq, rows, DH), bf),
                pltpu.VMEM((NY, heads, rows, DH), bf),
                pltpu.VMEM((NY, heads, rows, DH), bf),
                pltpu.VMEM((rows, width), f32),
                pltpu.VMEM((2, chans, G), bf),
                pltpu.VMEM((2, chans, G), bf),
                pltpu.VMEM((8, seq * rows), f32),
                DMA((NY, 2)),
                DMA((2,)),
                DMA((6,)),
                DMA((2, R)),
                DMA((2, 2, 2, half)),
                DMA((2, 2, 2, half)),
                DMA((4,)),
                DMA((4,)),
                DMA((3, NY)),
                DMA((NY, NY)),
                DMA((2, NY)),
                DMA((2, seq)),
                DMA((4,)),
                DMA((NY,)),
                DMA((2,)),
                DMA((2,)),
            ],
            compiler_params=pltpu.CompilerParams(
                collective_id=0, has_side_effects=True, vmem_limit_bytes=60 * 1024 * 1024
            ),
            name="block",
        )(
            hidden[0, 0],
            w_qkv,
            w_out,
            jnp.transpose(modulation, (1, 0, 2)),
            q_gain,
            k_gain,
            w_head.T,
            lengths,
            guidance,
            step_size,
        )
        return (latent[0].T - change).T[None]

    return jax.shard_map(
        local,
        mesh=mesh,
        in_specs=(
            P("cfg", "req", "seq", None),
            P("req", "seq", "cfg"),
            P("req", None, None),
            P("req", None),
            P("req", None),
            P(),
            P(),
            P(),
            P("req"),
            P("req"),
            P("req"),
        ),
        out_specs=P("req", "seq", "cfg"),
        check_vma=False,
    )
```
